32 devices in a mesh: tm: 4 (over x, core), sky: 8 (over z, y).
Axes of the slice: x: 2, y: 2, z: 4, core: 2. Of those that a mesh axis runs over, the one named last changes fastest.
Arguments:
- residual: bfloat16 [64, 256, 2048], P('tm', 'sky'), may hold values from -6 to 6
- point_spread: bfloat16 [11, 11], replicated, may hold values from 0.0019989014 to 0.049804688
- star_row: int32 [2048], P('sky'), may hold values from 0 to 255, as said below
- star_col: int32 [2048], P('sky'), may hold values from 0 to 2047
- star_flux: float32 [2048], P('sky'), may hold values from 0.5 to 4
- transit_depth: float32 [2048], P('sky'), may hold values from 0.1 to 0.9
- transit_flag: int32 [64, 2048], P('tm', 'sky'), may hold values 0 or 1
Outputs:
- grid_grad: float32 [256, 2048], P('sky', 'tm')
- flux_grad: float32 [2048], P('sky')
- depth_grad: float32 [2048], P('sky')
The draws below stay inside these ranges and needn't reach their ends.
Inputs may be any that keep to these rules, and one draw needn't show every extreme that they name: `star_row`: star s lies in rows (s // 256) * 32 to (s // 256) * 32 + 31.
All inputs are finite; a program needn't handle non-finite values. No bound on the sum of `transit_flag` on one device may be relied on, other than what follows from the above.
Results may differ from the reference program's by a relative error of at most 0.0003.
Values may be sent and summed in bfloat16 or wider, within the bound.
A program may use at most 320 MiB of HBM per device.

```python
import math
import jax
import jax.numpy as jnp
from jax import lax

NX = 2048
PSF_W = 11
ROWS = 32
STAR_DEV = 256
NY = 256
CAD = 64
NSTARS = 2048


def draw_star_row(key, part):
    owners = jnp.arange(NSTARS, dtype=jnp.int32) // STAR_DEV
    offsets = jax.random.randint(key, (NSTARS,), 0, ROWS, dtype=jnp.int32)
    return (owners * ROWS + offsets).astype(jnp.int32)


def with_ends(entries, own_key, smallest, largest):
    spot = [jax.random.randint(jax.random.fold_in(own_key, axis), (), 0, length) for axis, length in enumerate(entries.shape)]
    longest = entries.shape.index(max(entries.shape))
    next_to = spot[:longest] + [(spot[longest] + 1) % entries.shape[longest]] + spot[longest + 1:]
    return entries.at[tuple(spot)].set(smallest).at[tuple(next_to)].set(largest)


def steps_of(stream_key, shape, cuts, least, high):
    gain = 1.0
    for axis_at, shards_of in cuts:
        draws = jax.random.uniform(jax.random.fold_in(jax.random.fold_in(stream_key, 6), axis_at), (shards_of,), jnp.float32, least / len(cuts), high / len(cuts))
        gain = gain * jnp.repeat(jnp.exp(draws), shape[axis_at] // shards_of).reshape((-1,) + (1,) * (len(shape) - 1 - axis_at))
    return gain


def normal_values(stream_key, dims, scale, bound, pieces=(), kind=jnp.bfloat16):
    drawn = jax.random.normal(stream_key, dims, jnp.float32) * scale
    if len(pieces) > 0:
        drawn = steps_of(stream_key, dims, pieces, -0.22, 0.18) * drawn
    return jnp.clip(drawn, min=-bound, max=bound).astype(kind)


def setup_inputs(seed: int = 0) -> dict:
    key_of = jax.random.split(jax.random.key(seed), 8)
    return {
        "residual": normal_values(key_of[0], (CAD, NY, NX), 1.0, 6.0, ((0, 4), (1, 8))),
        "point_spread": jnp.clip(jnp.exp(jax.random.uniform(key_of[1], (PSF_W, PSF_W), jnp.float32, math.log(0.0019989014), math.log(0.049804688))), 0.0019989014, 0.049804688).astype(jnp.bfloat16),
        "star_row": draw_star_row(jax.random.fold_in(key_of[7], 71), 0),
        "star_col": with_ends(jax.random.randint(key_of[3], (NSTARS,), 0, NX), jax.random.fold_in(key_of[3], 1), 0, NX - 1).astype(jnp.int32),
        "star_flux": jnp.clip(jnp.exp(math.log(4.0) - 2.0794415 * jax.random.uniform(key_of[4], (NSTARS,), jnp.float32) ** steps_of(key_of[4], (NSTARS,), ((0, 8),), -0.2, 0.2)), 0.5, 4.0),
        "transit_depth": jnp.clip(jnp.exp(math.log(0.9) - 2.1972245 * jax.random.uniform(key_of[5], (NSTARS,), jnp.float32) ** steps_of(key_of[5], (NSTARS,), ((0, 8),), -0.2, 0.2)), 0.1, 0.9),
        "transit_flag": with_ends((jax.random.randint(key_of[6], (CAD, NSTARS), 0, 3) < 1).astype(jnp.int32), jax.random.fold_in(key_of[6], 1), 0, 1),
    }


def reference(residual, point_spread, star_row, star_col, star_flux, transit_depth, transit_flag):
    spread = point_spread.astype(jnp.float32)
    margin = (PSF_W - 1) // 2

    def one_cadence(grid_sum, frame):
        field = jnp.pad(frame.astype(jnp.float32), margin)
        correlated = jnp.zeros((NY, NX), jnp.float32)
        for across in range(PSF_W):
            for along in range(PSF_W):
                correlated = correlated + spread[across, along] * field[across:across + NY, along:along + NX]
        return grid_sum + correlated, correlated[star_row, star_col]

    grid_grad, at_stars = lax.scan(one_cadence, jnp.zeros((NY, NX), jnp.float32), residual)
    flags = transit_flag.astype(jnp.float32)
    flux_grad = jnp.sum((1.0 - transit_depth[None, :] * flags) * at_stars, axis=0)
    depth_grad = -star_flux * jnp.sum(flags * at_stars, axis=0)
    return grid_grad, flux_grad, depth_grad
```

```python
import functools
import jax
import jax.numpy as jnp
from jax import lax
from jax.experimental import pallas as pl
from jax.experimental.pallas import tpu as pltpu
from jax.sharding import PartitionSpec as P

LANES = 128
PAD = 8


def local_kernel(
    stars_ref, psf_ref, res_ref, flags_ref, grid_ref, part_ref,
    flat, windows, table, wide, gathered, dense, summed, split,
):
    times, rows, columns = res_ref.shape
    width = psf_ref.shape[0]
    margin = (width - 1) // 2
    blocks = columns // LANES
    halves = rows // 16
    star_count = stars_ref.shape[1]
    tall = rows + 2 * margin

    span = 144
    gap = lax.broadcasted_iota(jnp.int32, (span, LANES), 0) - lax.broadcasted_iota(
        jnp.int32, (span, LANES), 1
    )
    for a in range(width):
        entry = jnp.zeros((span, LANES), jnp.float32)
        for b in range(width):
            entry = jnp.where(gap == b, psf_ref[a, b], entry)
        entry = entry.astype(jnp.bfloat16)
        table[pl.ds(a * LANES, LANES), :] = entry[:LANES]
        wide[pl.ds(0, span), pl.ds(a * LANES, LANES)] = entry
    wide[pl.ds(span, 256 - span), :] = jnp.zeros((256 - span, width * LANES), jnp.bfloat16)

    zero_side = jnp.zeros((rows, LANES), jnp.float32)
    summed[:, pl.ds(0, LANES)] = zero_side
    summed[:, pl.ds(LANES + columns, LANES)] = zero_side
    summed[:, pl.ds(2 * LANES + columns, LANES)] = zero_side

    @pl.loop(0, blocks)
    def _(b):
        at = pl.ds(pl.multiple_of(b * LANES, LANES), LANES)
        total = res_ref[0, :, at].astype(jnp.float32)
        for t in range(1, times):
            total = total + res_ref[t, :, at].astype(jnp.float32)
        summed[:, pl.ds(pl.multiple_of((b + 1) * LANES, LANES), LANES)] = total

    grid_ref[...] = jnp.zeros_like(grid_ref)
    group = 4

    @pl.loop(0, blocks // group)
    def _(g):
        for i in range(group):
            start = pl.multiple_of((g * group + i) * LANES, LANES)
            window = summed[:, pl.ds(start, 3 * LANES)]
            moved = pltpu.roll(window, margin, 1)[:, LANES:]
            high = moved.astype(jnp.bfloat16)
            low = (moved - high.astype(jnp.float32)).astype(jnp.bfloat16)
            split[pl.ds(2 * i * rows, rows), :] = high
            split[pl.ds((2 * i + 1) * rows, rows), :] = low
        for a in range(width):
            product = jnp.dot(
                split[...], wide[:, pl.ds(a * LANES, LANES)], preferred_element_type=jnp.float32
            )
            for i in range(group):
                start = pl.multiple_of((g * group + i) * LANES, LANES)
                term = product[2 * i * rows : (2 * i + 1) * rows] + product[
                    (2 * i + 1) * rows : (2 * i + 2) * rows
                ]
                grid_ref[pl.ds(PAD + margin - a, rows), pl.ds(start, LANES)] += term

    flat[:, pl.ds(0, LANES)] = jnp.zeros((256, LANES), jnp.float32)
    flat[:, pl.ds(LANES + columns, LANES)] = jnp.zeros((256, LANES), jnp.float32)
    first = lax.broadcasted_iota(jnp.int32, (256, 256), 0)
    second = lax.broadcasted_iota(jnp.int32, (256, 256), 1)
    swap = (first == (second % 16) * 16 + second // 16).astype(jnp.bfloat16)
    windows[:, pl.ds(0, margin)] = jnp.zeros((2 * blocks, margin, 16, LANES), jnp.bfloat16)
    windows[:, pl.ds(margin + rows, margin)] = jnp.zeros(
        (2 * blocks, margin, 16, LANES), jnp.bfloat16
    )
    for h in range(halves):

        @pl.loop(0, columns // 256)
        def _(c):
            at = pl.ds(pl.multiple_of(c * 256, 256), 256)
            piece = res_ref[:, pl.ds(16 * h, 16), at].reshape(256, 256)
            flat[:, pl.ds(pl.multiple_of(c * 256 + LANES, LANES), 256)] = jnp.dot(
                swap, piece, preferred_element_type=jnp.float32
            )

        @pl.loop(0, blocks)
        def _(b):
            start = pl.multiple_of(b * LANES, LANES)
            left = flat[:, pl.ds(start, 2 * LANES)]
            right = flat[:, pl.ds(pl.multiple_of(start + LANES, LANES), 2 * LANES)]
            near = pltpu.roll(left, margin, 1)[:, LANES:]
            far = pltpu.roll(right, 2 * LANES - (64 - margin), 1)[:, :LANES]
            rows_at = pl.ds(margin + 16 * h, 16)
            windows[b, rows_at] = near.astype(jnp.bfloat16).reshape(16, 16, LANES)
            windows[blocks + b, rows_at] = far.astype(jnp.bfloat16).reshape(16, 16, LANES)

    lane = lax.broadcasted_iota(jnp.int32, (16, LANES), 1)
    lowest = lax.axis_index("sky") * rows
    for which, (first_tap, taps) in enumerate(((0, width), (width - margin, margin), (0, margin))):
        base = first_tap
        last = tall - taps

        def chunk(g, c, slot, acc):
            for s in range(16):
                star = g * LANES + c * 16 + s
                row = stars_ref[2 * which, star] - lowest + base
                row = jnp.clip(row, 0, last)
                column = stars_ref[2 * which + 1, star]
                block = column // LANES + blocks * ((column // 64) % 2)
                found = windows[block, pl.ds(row, taps)]
                for a in range(taps):
                    gathered[slot, pl.ds(16 * s, 16), pl.ds(a * LANES, LANES)] = found[a]
            dense[slot] = jnp.dot(
                gathered[slot, :, pl.ds(0, taps * LANES)],
                table[pl.ds(first_tap * LANES, taps * LANES), :],
                preferred_element_type=jnp.float32,
            )
            for s in range(16):
                star = g * LANES + c * 16 + s
                place = c * 16 + s
                offset = stars_ref[2 * which + 1, star] % 64
                moved = pltpu.roll(
                    dense[slot, pl.ds(16 * s, 16), :], (place - offset + LANES) % LANES, 1
                )
                acc = jnp.where(lane == place, moved, acc)
            return acc

        for g in range(star_count // LANES):

            def pair(c, acc, g=g):
                acc = chunk(g, 2 * c, 0, acc)
                return chunk(g, 2 * c + 1, 1, acc)

            acc = lax.fori_loop(0, LANES // 32, pair, jnp.zeros((16, LANES), jnp.float32))
            at = pl.ds(g * LANES, LANES)
            part_ref[pl.ds(2 * which, 1), at] = jnp.sum(acc, axis=0, keepdims=True)
            part_ref[pl.ds(2 * which + 1, 1), at] = jnp.sum(
                acc * flags_ref[which, :, at], axis=0, keepdims=True
            )


def local_parts(stars, spread, residual, flags):
    times, rows, columns = residual.shape
    width = spread.shape[0]
    margin = (width - 1) // 2
    blocks = columns // LANES
    count = stars.shape[1]
    vmem = pl.BlockSpec(memory_space=pltpu.VMEM)
    smem = pl.BlockSpec(memory_space=pltpu.SMEM)
    return pl.pallas_call(
        local_kernel,
        out_shape=(
            jax.ShapeDtypeStruct((rows + 2 * PAD, columns), jnp.float32),
            jax.ShapeDtypeStruct((8, count), jnp.float32),
        ),
        in_specs=[smem, smem, vmem, vmem],
        out_specs=(vmem, vmem),
        scratch_shapes=[
            pltpu.VMEM((256, columns + 2 * LANES), jnp.float32),
            pltpu.VMEM((2 * blocks, rows + 2 * margin, 16, LANES), jnp.bfloat16),
            pltpu.VMEM((width * LANES, LANES), jnp.bfloat16),
            pltpu.VMEM((256, width * LANES), jnp.bfloat16),
            pltpu.VMEM((2, 256, width * LANES), jnp.bfloat16),
            pltpu.VMEM((2, 256, LANES), jnp.float32),
            pltpu.VMEM((rows, columns + 3 * LANES), jnp.float32),
            pltpu.VMEM((8 * rows, 256), jnp.bfloat16),
        ],
        compiler_params=pltpu.CompilerParams(vmem_limit_bytes=40 << 20),
    )(stars, spread, residual, flags)


def per_device(residual, point_spread, star_row, star_col, star_flux, transit_depth, transit_flag):
    times, rows, columns = residual.shape
    size = lax.axis_size("sky")
    up = [(i, i + 1) for i in range(size - 1)]
    down = [(i + 1, i) for i in range(size - 1)]
    info = jnp.concatenate([star_row[None], star_col[None], transit_flag], axis=0)
    before = lax.ppermute(info, "sky", up)
    after = lax.ppermute(info, "sky", down)
    stars = jnp.concatenate([info[:2], before[:2], after[:2]], axis=0)
    flags = jnp.stack([info[2:], before[2:], after[2:]]).astype(jnp.float32)
    grid, part = local_parts(stars, point_spread.astype(jnp.float32), residual, flags)
    edge_count = PAD * columns
    to_before = jnp.concatenate([grid[:PAD].reshape(-1), part[2:4].reshape(-1)])
    to_after = jnp.concatenate([grid[PAD + rows :].reshape(-1), part[4:6].reshape(-1)])
    from_before = lax.ppermute(to_after, "sky", up)
    from_after = lax.ppermute(to_before, "sky", down)
    own = grid[PAD : PAD + rows]
    own = own.at[:PAD].add(from_before[:edge_count].reshape(PAD, columns))
    own = own.at[rows - PAD :].add(from_after[:edge_count].reshape(PAD, columns))
    sums = part[:2] + (from_before[edge_count:] + from_after[edge_count:]).reshape(2, -1)
    grid_share = lax.psum_scatter(own, "tm", scatter_dimension=1, tiled=True)
    sums = lax.psum(sums, "tm")
    return (grid_share, sums[0] - transit_depth * sums[1], -star_flux * sums[1])


def solution(mesh):
    in_specs = (P("tm", "sky", None), P(), P("sky"), P("sky"), P("sky"), P("sky"), P("tm", "sky"))
    out_specs = (P("sky", "tm"), P("sky"), P("sky"))
    return jax.shard_map(
        per_device, mesh=mesh, in_specs=in_specs, out_specs=out_specs, check_vma=False
    )
```

```python
import functools
import jax
import jax.numpy as jnp
from jax import lax
from jax.experimental import pallas as pl
from jax.experimental.pallas import tpu as pltpu
from jax.sharding import PartitionSpec as P

LANES = 128
PAD = 8


def kernel(
    stars_ref, psf_ref, res_ref, info_ref, flux_ref, depth_ref,
    share_ref, flux_grad_ref, depth_grad_ref,
    flat, windows, table, wide, gathered, dense, summed, split,
    comb, part, near_stars, got_info, got_main, got_edge, got_part, got_edge_part,
    info_send, info_recv, main_send, main_recv, edge_send, edge_recv,
    part_send, part_recv, edge_part_send, edge_part_recv, local_sem,
):
    times, rows, columns = res_ref.shape
    width = psf_ref.shape[0]
    margin = (width - 1) // 2
    blocks = columns // LANES
    halves = rows // 16
    star_count = stars_ref.shape[1]
    tall = rows + 2 * margin
    group_count, _, share = comb.shape
    me = lax.axis_index("tm")
    place_sky = lax.axis_index("sky")
    sky_size = lax.axis_size("sky")
    has = (place_sky > 0, place_sky < sky_size - 1)
    beside = (place_sky - 1, place_sky + 1)

    def to(tm, sky):
        return dict(device_id={"tm": tm, "sky": sky}, device_id_type=pl.DeviceIdType.MESH)

    def other(d):
        return lax.rem(me + d, group_count)

    barrier = pltpu.get_barrier_semaphore()
    for d in range(1, group_count):
        pl.semaphore_signal(barrier, inc=1, **to(other(d), place_sky))
    for side in range(2):

        @pl.when(has[side])
        def _(side=side):
            for d in range(group_count):
                pl.semaphore_signal(barrier, inc=1, **to(other(d), beside[side]))

    peers = group_count - 1
    for side in range(2):
        peers = peers + jnp.where(has[side], group_count, 0)
    pl.semaphore_wait(barrier, peers)

    def info_copy(side):
        return pltpu.make_async_remote_copy(
            src_ref=info_ref, dst_ref=got_info.at[1 - side],
            send_sem=info_send.at[side], recv_sem=info_recv.at[1 - side],
            **to(me, beside[side]),
        )

    def main_copy(d):
        return pltpu.make_async_remote_copy(
            src_ref=comb.at[other(d), pl.ds(PAD, rows)], dst_ref=got_main.at[d - 1],
            send_sem=main_send.at[d - 1], recv_sem=main_recv.at[d - 1],
            **to(other(d), place_sky),
        )

    def edge_copy(side, d):
        return pltpu.make_async_remote_copy(
            src_ref=comb.at[other(d), pl.ds((0, PAD + rows)[side], PAD)],
            dst_ref=got_edge.at[1 - side, d],
            send_sem=edge_send.at[side, d], recv_sem=edge_recv.at[1 - side, d],
            **to(other(d), beside[side]),
        )

    def part_copy(d):
        return pltpu.make_async_remote_copy(
            src_ref=part.at[0], dst_ref=got_part.at[d - 1],
            send_sem=part_send.at[d - 1], recv_sem=part_recv.at[d - 1],
            **to(other(d), place_sky),
        )

    def edge_part_copy(side, d):
        return pltpu.make_async_remote_copy(
            src_ref=part.at[1 + side], dst_ref=got_edge_part.at[1 - side, d],
            send_sem=edge_part_send.at[side, d], recv_sem=edge_part_recv.at[1 - side, d],
            **to(other(d), beside[side]),
        )

    for side in range(2):

        @pl.when(has[side])
        def _(side=side):
            info_copy(side).start()

    span = 144
    gap = lax.broadcasted_iota(jnp.int32, (span, LANES), 0) - lax.broadcasted_iota(
        jnp.int32, (span, LANES), 1
    )
    for a in range(width):
        entry = jnp.zeros((span, LANES), jnp.float32)
        for b in range(width):
            entry = jnp.where(gap == b, psf_ref[a, b], entry)
        entry = entry.astype(jnp.bfloat16)
        table[pl.ds(a * LANES, LANES), :] = entry[:LANES]
        wide[pl.ds(0, span), pl.ds(a * LANES, LANES)] = entry
    wide[pl.ds(span, 256 - span), :] = jnp.zeros((256 - span, width * LANES), jnp.bfloat16)

    zero_side = jnp.zeros((rows, LANES), jnp.float32)
    summed[:, pl.ds(0, LANES)] = zero_side
    summed[:, pl.ds(LANES + columns, LANES)] = zero_side
    summed[:, pl.ds(2 * LANES + columns, LANES)] = zero_side

    @pl.loop(0, blocks)
    def _(b):
        at = pl.ds(pl.multiple_of(b * LANES, LANES), LANES)
        total = res_ref[0, :, at].astype(jnp.float32)
        for t in range(1, times):
            total = total + res_ref[t, :, at].astype(jnp.float32)
        summed[:, pl.ds(pl.multiple_of((b + 1) * LANES, LANES), LANES)] = total

    group = share // LANES
    comb[...] = jnp.zeros_like(comb)

    @pl.loop(0, group_count)
    def _(g):
        for i in range(group):
            start = pl.multiple_of((g * group + i) * LANES, LANES)
            window = summed[:, pl.ds(start, 3 * LANES)]
            moved = pltpu.roll(window, margin, 1)[:, LANES:]
            high = moved.astype(jnp.bfloat16)
            low = (moved - high.astype(jnp.float32)).astype(jnp.bfloat16)
            split[pl.ds(2 * i * rows, rows), :] = high
            split[pl.ds((2 * i + 1) * rows, rows), :] = low
        for a in range(width):
            product = jnp.dot(
                split[...], wide[:, pl.ds(a * LANES, LANES)], preferred_element_type=jnp.float32
            )
            for i in range(group):
                term = product[2 * i * rows : (2 * i + 1) * rows] + product[
                    (2 * i + 1) * rows : (2 * i + 2) * rows
                ]
                comb[g, pl.ds(PAD + margin - a, rows), pl.ds(i * LANES, LANES)] += term

    for d in range(1, group_count):
        main_copy(d).start()
    for side in range(2):

        @pl.when(has[side])
        def _(side=side):
            for d in range(group_count):
                edge_copy(side, d).start()

    flat[:, pl.ds(0, LANES)] = jnp.zeros((256, LANES), jnp.float32)
    flat[:, pl.ds(LANES + columns, LANES)] = jnp.zeros((256, LANES), jnp.float32)
    first = lax.broadcasted_iota(jnp.int32, (256, 256), 0)
    second = lax.broadcasted_iota(jnp.int32, (256, 256), 1)
    swap = (first == (second % 16) * 16 + second // 16).astype(jnp.bfloat16)
    windows[:, pl.ds(0, margin)] = jnp.zeros((2 * blocks, margin, 16, LANES), jnp.bfloat16)
    windows[:, pl.ds(margin + rows, margin)] = jnp.zeros(
        (2 * blocks, margin, 16, LANES), jnp.bfloat16
    )
    for h in range(halves):

        @pl.loop(0, columns // 256)
        def _(c):
            at = pl.ds(pl.multiple_of(c * 256, 256), 256)
            piece = res_ref[:, pl.ds(16 * h, 16), at].reshape(256, 256)
            flat[:, pl.ds(pl.multiple_of(c * 256 + LANES, LANES), 256)] = jnp.dot(
                swap, piece, preferred_element_type=jnp.float32
            )

        @pl.loop(0, blocks)
        def _(b):
            start = pl.multiple_of(b * LANES, LANES)
            left = flat[:, pl.ds(start, 2 * LANES)]
            right = flat[:, pl.ds(pl.multiple_of(start + LANES, LANES), 2 * LANES)]
            near = pltpu.roll(left, margin, 1)[:, LANES:]
            far = pltpu.roll(right, 2 * LANES - (64 - margin), 1)[:, :LANES]
            rows_at = pl.ds(margin + 16 * h, 16)
            windows[b, rows_at] = near.astype(jnp.bfloat16).reshape(16, 16, LANES)
            windows[blocks + b, rows_at] = far.astype(jnp.bfloat16).reshape(16, 16, LANES)

    lane = lax.broadcasted_iota(jnp.int32, (16, LANES), 1)
    lowest = place_sky * rows
    part[...] = jnp.zeros_like(part)

    def stars_part(which, first_tap, taps, star_row, star_col, flags):
        last = tall - taps

        def chunk(g, c, slot, acc):
            for s in range(16):
                star = g * LANES + c * 16 + s
                row = jnp.clip(star_row(star) - lowest + first_tap, 0, last)
                column = star_col(star)
                block = column // LANES + blocks * ((column // 64) % 2)
                found = windows[block, pl.ds(row, taps)]
                for a in range(taps):
                    gathered[slot, pl.ds(16 * s, 16), pl.ds(a * LANES, LANES)] = found[a]
            dense[slot] = jnp.dot(
                gathered[slot, :, pl.ds(0, taps * LANES)],
                table[pl.ds(first_tap * LANES, taps * LANES), :],
                preferred_element_type=jnp.float32,
            )
            for s in range(16):
                star = g * LANES + c * 16 + s
                place = c * 16 + s
                offset = star_col(star) % 64
                moved = pltpu.roll(
                    dense[slot, pl.ds(16 * s, 16), :], (place - offset + LANES) % LANES, 1
                )
                acc = jnp.where(lane == place, moved, acc)
            return acc

        for g in range(star_count // LANES):

            def pair(c, acc, g=g):
                acc = chunk(g, 2 * c, 0, acc)
                return chunk(g, 2 * c + 1, 1, acc)

            acc = lax.fori_loop(0, LANES // 32, pair, jnp.zeros((16, LANES), jnp.float32))
            at = pl.ds(g * LANES, LANES)
            part[which, pl.ds(0, 1), at] = jnp.sum(acc, axis=0, keepdims=True)
            part[which, pl.ds(1, 1), at] = jnp.sum(
                acc * flags(at).astype(jnp.float32), axis=0, keepdims=True
            )

    stars_part(
        0, 0, width,
        lambda n: stars_ref[0, n], lambda n: stars_ref[1, n],
        lambda at: info_ref[pl.ds(8, times), at],
    )
    for d in range(1, group_count):
        part_copy(d).start()
    for side in range(2):

        @pl.when(has[side])
        def _(side=side):
            info_copy(1 - side).wait_recv()
            fetch = pltpu.make_async_copy(
                got_info.at[side, pl.ds(0, 8)], near_stars.at[side], local_sem
            )
            fetch.start()
            fetch.wait()
            stars_part(
                1 + side, (width - margin, 0)[side], margin,
                lambda n: near_stars[side, 0, n], lambda n: near_stars[side, 1, n],
                lambda at: got_info[side, pl.ds(8, times), at],
            )
            for d in range(group_count):
                edge_part_copy(side, d).start()

    for d in range(1, group_count):
        main_copy(d).wait_recv()
    total = comb[me, pl.ds(PAD, rows)]
    for d in range(1, group_count):
        total = total + got_main[d - 1]
    share_ref[...] = total
    for side in range(2):

        @pl.when(has[side])
        def _(side=side):
            for d in range(group_count):
                edge_copy(1 - side, d).wait_recv()
            edge = got_edge[side, 0]
            for d in range(1, group_count):
                edge = edge + got_edge[side, d]
            share_ref[pl.ds((0, rows - PAD)[side], PAD), :] += edge

    for d in range(1, group_count):
        part_copy(d).wait_recv()
    sums = part[0]
    for d in range(1, group_count):
        sums = sums + got_part[d - 1]
    flux_grad_ref[...] = sums[0:1]
    depth_grad_ref[...] = sums[1:2]
    for side in range(2):

        @pl.when(has[side])
        def _(side=side):
            for d in range(group_count):
                edge_part_copy(1 - side, d).wait_recv()
            edge = got_edge_part[side, 0]
            for d in range(1, group_count):
                edge = edge + got_edge_part[side, d]
            flux_grad_ref[...] += edge[0:1]
            depth_grad_ref[...] += edge[1:2]

    flux_grad_ref[...] = flux_grad_ref[...] - depth_ref[...] * depth_grad_ref[...]
    depth_grad_ref[...] = -flux_ref[...] * depth_grad_ref[...]
    for d in range(1, group_count):
        main_copy(d).wait_send()
        part_copy(d).wait_send()
    for side in range(2):

        @pl.when(has[side])
        def _(side=side):
            info_copy(side).wait_send()
            for d in range(group_count):
                edge_copy(side, d).wait_send()
                edge_part_copy(side, d).wait_send()


def per_device(residual, point_spread, star_row, star_col, star_flux, transit_depth, transit_flag):
    times, rows, columns = residual.shape
    width = point_spread.shape[0]
    margin = (width - 1) // 2
    blocks = columns // LANES
    count = star_row.shape[0]
    groups = lax.axis_size("tm")
    share = columns // groups
    stars = jnp.stack([star_row, star_col])
    info = jnp.concatenate([stars, jnp.zeros((6, count), jnp.int32), transit_flag], axis=0)
    vmem = pl.BlockSpec(memory_space=pltpu.VMEM)
    smem = pl.BlockSpec(memory_space=pltpu.SMEM)
    dma = pltpu.SemaphoreType.DMA
    grid_share, flux_grad, depth_grad = pl.pallas_call(
        kernel,
        out_shape=(
            jax.ShapeDtypeStruct((rows, share), jnp.float32),
            jax.ShapeDtypeStruct((1, count), jnp.float32),
            jax.ShapeDtypeStruct((1, count), jnp.float32),
        ),
        in_specs=[smem, smem, vmem, vmem, vmem, vmem],
        out_specs=(vmem, vmem, vmem),
        scratch_shapes=[
            pltpu.VMEM((256, columns + 2 * LANES), jnp.float32),
            pltpu.VMEM((2 * blocks, rows + 2 * margin, 16, LANES), jnp.bfloat16),
            pltpu.VMEM((width * LANES, LANES), jnp.bfloat16),
            pltpu.VMEM((256, width * LANES), jnp.bfloat16),
            pltpu.VMEM((2, 256, width * LANES), jnp.bfloat16),
            pltpu.VMEM((2, 256, LANES), jnp.float32),
            pltpu.VMEM((rows, columns + 3 * LANES), jnp.float32),
            pltpu.VMEM((2 * rows * (share // LANES), 256), jnp.bfloat16),
            pltpu.VMEM((groups, rows + 2 * PAD, share), jnp.float32),
            pltpu.VMEM((3, 8, count), jnp.float32),
            pltpu.SMEM((2, 8, count), jnp.int32),
            pltpu.VMEM((2, 8 + times, count), jnp.int32),
            pltpu.VMEM((groups - 1, rows, share), jnp.float32),
            pltpu.VMEM((2, groups, PAD, share), jnp.float32),
            pltpu.VMEM((groups - 1, 8, count), jnp.float32),
            pltpu.VMEM((2, groups, 8, count), jnp.float32),
            dma((2,)), dma((2,)), dma((groups - 1,)), dma((groups - 1,)),
            dma((2, groups)), dma((2, groups)), dma((groups - 1,)), dma((groups - 1,)),
            dma((2, groups)), dma((2, groups)), dma,
        ],
        compiler_params=pltpu.CompilerParams(
            collective_id=0, has_side_effects=True, vmem_limit_bytes=48 << 20
        ),
    )(stars, point_spread.astype(jnp.float32), residual, info, star_flux[None], transit_depth[None])
    return grid_share, flux_grad[0], depth_grad[0]


def solution(mesh):
    in_specs = (P("tm", "sky", None), P(), P("sky"), P("sky"), P("sky"), P("sky"), P("tm", "sky"))
    out_specs = (P("sky", "tm"), P("sky"), P("sky"))
    return jax.shard_map(
        per_device, mesh=mesh, in_specs=in_specs, out_specs=out_specs, check_vma=False
    )
```

```python
import functools
import jax
import jax.numpy as jnp
from jax import lax
from jax.experimental import pallas as pl
from jax.experimental.pallas import tpu as pltpu
from jax.sharding import PartitionSpec as P

LANES = 128
PAD = 8


def kernel(
    psf_hbm, res_hbm, row_hbm, col_hbm, flag_hbm,
    share_ref, plain_ref, flagged_ref,
    psf_ref, res_ref, stars, flags, codes, lookup,
    flat, windows, table, wide, gathered, dense, summed, split,
    comb, part, got_main, got_edge, got_part, got_edge_part,
    info_send, info_recv, main_send, main_recv, edge_send, edge_recv,
    part_send, part_recv, edge_part_send, edge_part_recv, local_sem, lookup_sem,
):
    times, rows, columns = res_ref.shape
    width = psf_ref.shape[0]
    margin = (width - 1) // 2
    blocks = columns // LANES
    halves = rows // 16
    star_count = row_hbm.shape[1]
    tall = rows + 2 * margin
    group_count, _, share = comb.shape
    me = lax.axis_index("tm")
    place_sky = lax.axis_index("sky")
    sky_size = lax.axis_size("sky")
    has = (place_sky > 0, place_sky < sky_size - 1)
    beside = (place_sky - 1, place_sky + 1)

    def to(tm, sky):
        return dict(device_id={"tm": tm, "sky": sky}, device_id_type=pl.DeviceIdType.MESH)

    def other(d):
        return lax.rem(me + d, group_count)

    barrier = pltpu.get_barrier_semaphore()
    for d in range(1, group_count):
        pl.semaphore_signal(barrier, inc=1, **to(other(d), place_sky))
    for side in range(2):

        @pl.when(has[side])
        def _(side=side):
            for d in range(group_count):
                pl.semaphore_signal(barrier, inc=1, **to(other(d), beside[side]))

    loads = [
        pltpu.make_async_copy(source, target, local_sem.at[n])
        for n, (source, target) in enumerate(
            (
                (psf_hbm, psf_ref),
                (row_hbm, stars.at[0, 0]),
                (col_hbm, stars.at[0, 1]),
                (flag_hbm, flags.at[0]),
                (res_hbm, res_ref),
            )
        )
    ]
    for load in loads:
        load.start()

    peers = group_count - 1
    for side in range(2):
        peers = peers + jnp.where(has[side], group_count, 0)
    pl.semaphore_wait(barrier, peers)

    def info_copies(side):
        other_side = 1 - side
        return [
            pltpu.make_async_remote_copy(
                src_ref=source, dst_ref=target,
                send_sem=info_send.at[side, n], recv_sem=info_recv.at[other_side, n],
                **to(me, beside[side]),
            )
            for n, (source, target) in enumerate(
                (
                    (row_hbm, stars.at[1 + other_side, 0]),
                    (col_hbm, stars.at[1 + other_side, 1]),
                    (flag_hbm, flags.at[1 + other_side]),
                )
            )
        ]

    def main_copy(d):
        return pltpu.make_async_remote_copy(
            src_ref=comb.at[other(d), pl.ds(PAD, rows)], dst_ref=got_main.at[d - 1],
            send_sem=main_send.at[d - 1], recv_sem=main_recv.at[d - 1],
            **to(other(d), place_sky),
        )

    def edge_copy(side, d):
        return pltpu.make_async_remote_copy(
            src_ref=comb.at[other(d), pl.ds((0, PAD + rows)[side], PAD)],
            dst_ref=got_edge.at[1 - side, d],
            send_sem=edge_send.at[side, d], recv_sem=edge_recv.at[1 - side, d],
            **to(other(d), beside[side]),
        )

    def part_copy(d):
        return pltpu.make_async_remote_copy(
            src_ref=part.at[0], dst_ref=got_part.at[d - 1],
            send_sem=part_send.at[d - 1], recv_sem=part_recv.at[d - 1],
            **to(other(d), place_sky),
        )

    def edge_part_copy(side, d):
        return pltpu.make_async_remote_copy(
            src_ref=part.at[1 + side], dst_ref=got_edge_part.at[1 - side, d],
            send_sem=edge_part_send.at[side, d], recv_sem=edge_part_recv.at[1 - side, d],
            **to(other(d), beside[side]),
        )

    for side in range(2):

        @pl.when(has[side])
        def _(side=side):
            for copy in info_copies(side):
                copy.start()

    lowest = place_sky * rows

    def taps_of(which):
        return ((0, width), (width - margin, margin), (0, margin))[which]

    def look_up(which):
        first_tap, taps = taps_of(which)
        row = jnp.clip(stars[which, 0] - lowest + first_tap, 0, tall - taps)
        column = stars[which, 1]
        block = lax.shift_right_logical(column, 7) + blocks * (
            lax.shift_right_logical(column, 6) & 1
        )
        codes[which, 0] = block * tall + row
        position = lax.broadcasted_iota(jnp.int32, (1, star_count), 1)
        codes[which, 1] = (position - (column & 63)) & (LANES - 1)
        return pltpu.make_async_copy(codes.at[which], lookup.at[which], lookup_sem.at[which])

    loads[1].wait()
    loads[2].wait()
    own_lookup = look_up(0)
    own_lookup.start()
    loads[0].wait()
    spread = psf_ref[...].astype(jnp.float32)

    span = 144
    gap = lax.broadcasted_iota(jnp.int32, (span, LANES), 0) - lax.broadcasted_iota(
        jnp.int32, (span, LANES), 1
    )
    for a in range(width):
        entry = jnp.zeros((span, LANES), jnp.float32)
        for b in range(width):
            entry = jnp.where(gap == b, spread[a : a + 1, b : b + 1], entry)
        entry = entry.astype(jnp.bfloat16)
        table[pl.ds(a * LANES, LANES), :] = entry[:LANES]
        wide[pl.ds(0, span), pl.ds(a * LANES, LANES)] = entry
    wide[pl.ds(span, 256 - span), :] = jnp.zeros((256 - span, width * LANES), jnp.bfloat16)

    loads[4].wait()
    zero_side = jnp.zeros((rows, LANES), jnp.float32)
    summed[:, pl.ds(0, LANES)] = zero_side
    summed[:, pl.ds(LANES + columns, LANES)] = zero_side
    summed[:, pl.ds(2 * LANES + columns, LANES)] = zero_side

    @pl.loop(0, blocks)
    def _(b):
        at = pl.ds(pl.multiple_of(b * LANES, LANES), LANES)
        total = res_ref[0, :, at].astype(jnp.float32)
        for t in range(1, times):
            total = total + res_ref[t, :, at].astype(jnp.float32)
        summed[:, pl.ds(pl.multiple_of((b + 1) * LANES, LANES), LANES)] = total

    group = share // LANES
    comb[...] = jnp.zeros_like(comb)

    @pl.loop(0, group_count)
    def _(g):
        for i in range(group):
            start = pl.multiple_of((g * group + i) * LANES, LANES)
            window = summed[:, pl.ds(start, 3 * LANES)]
            moved = pltpu.roll(window, margin, 1)[:, LANES:]
            high = moved.astype(jnp.bfloat16)
            low = (moved - high.astype(jnp.float32)).astype(jnp.bfloat16)
            split[pl.ds(2 * i * rows, rows), :] = high
            split[pl.ds((2 * i + 1) * rows, rows), :] = low
        for a in range(width):
            product = jnp.dot(
                split[...], wide[:, pl.ds(a * LANES, LANES)], preferred_element_type=jnp.float32
            )
            for i in range(group):
                term = product[2 * i * rows : (2 * i + 1) * rows] + product[
                    (2 * i + 1) * rows : (2 * i + 2) * rows
                ]
                comb[g, pl.ds(PAD + margin - a, rows), pl.ds(i * LANES, LANES)] += term

    for d in range(1, group_count):
        main_copy(d).start()
    for side in range(2):

        @pl.when(has[side])
        def _(side=side):
            for d in range(group_count):
                edge_copy(side, d).start()

    flat[:, pl.ds(0, LANES)] = jnp.zeros((256, LANES), jnp.float32)
    flat[:, pl.ds(LANES + columns, LANES)] = jnp.zeros((256, LANES), jnp.float32)
    first = lax.broadcasted_iota(jnp.int32, (256, 256), 0)
    second = lax.broadcasted_iota(jnp.int32, (256, 256), 1)
    swap = (first == (second % 16) * 16 + second // 16).astype(jnp.bfloat16)
    for b in range(2 * blocks):
        for r in (b * tall, b * tall + margin + rows):
            windows[pl.ds(r, margin)] = jnp.zeros((margin, 16, LANES), jnp.bfloat16)
    for h in range(halves):

        @pl.loop(0, columns // 256)
        def _(c):
            at = pl.ds(pl.multiple_of(c * 256, 256), 256)
            piece = res_ref[:, pl.ds(16 * h, 16), at].reshape(256, 256)
            flat[:, pl.ds(pl.multiple_of(c * 256 + LANES, LANES), 256)] = jnp.dot(
                swap, piece, preferred_element_type=jnp.float32
            )

        @pl.loop(0, blocks // 4)
        def _(c):
            start = pl.multiple_of(c * 4 * LANES, LANES)
            left = flat[:, pl.ds(start, 5 * LANES)]
            right = flat[:, pl.ds(pl.multiple_of(start + LANES, LANES), 5 * LANES)]
            near = pltpu.roll(left, margin, 1).astype(jnp.bfloat16)
            far = pltpu.roll(right, 5 * LANES - (64 - margin), 1).astype(jnp.bfloat16)
            for i in range(4):
                b = c * 4 + i
                windows[pl.ds(b * tall + margin + 16 * h, 16)] = near[
                    :, (i + 1) * LANES : (i + 2) * LANES
                ].reshape(16, 16, LANES)
                windows[pl.ds((blocks + b) * tall + margin + 16 * h, 16)] = far[
                    :, i * LANES : (i + 1) * LANES
                ].reshape(16, 16, LANES)

    lane = lax.broadcasted_iota(jnp.int32, (16, LANES), 1)
    part[...] = jnp.zeros_like(part)
    slots = gathered.shape[0]

    def stars_part(which):
        first_tap, taps = taps_of(which)
        for g in range(star_count // LANES):

            def gather(c, slot, g=g):
                for s in range(16):
                    found = windows[pl.ds(lookup[which, 0, 0, g * LANES + c * 16 + s], taps)]
                    for a in range(taps):
                        gathered[slot, pl.ds(16 * s, 16), pl.ds(a * LANES, LANES)] = found[a]

            def multiply(slot):
                dense[slot] = jnp.dot(
                    gathered[slot, :, pl.ds(0, taps * LANES)],
                    table[pl.ds(first_tap * LANES, taps * LANES), :],
                    preferred_element_type=jnp.float32,
                )

            def select(c, slot, acc, g=g):
                for s in range(16):
                    moved = pltpu.roll(
                        dense[slot, pl.ds(16 * s, 16), :],
                        lookup[which, 1, 0, g * LANES + c * 16 + s],
                        1,
                    )
                    acc = jnp.where(lane == c * 16 + s, moved, acc)
                return acc

            def some(c, acc):
                for n in range(slots + 2):
                    if n < slots:
                        gather(slots * c + n, n)
                        multiply(n)
                    if n >= 2:
                        acc = select(slots * c + n - 2, n - 2, acc)
                return acc

            acc = lax.fori_loop(
                0, LANES // (16 * slots), some, jnp.zeros((16, LANES), jnp.float32)
            )
            at = pl.ds(g * LANES, LANES)
            part[which, pl.ds(0, 1), at] = jnp.sum(acc, axis=0, keepdims=True)
            part[which, pl.ds(1, 1), at] = jnp.sum(
                acc * flags[which, :, at].astype(jnp.float32), axis=0, keepdims=True
            )

    own_lookup.wait()
    loads[3].wait()
    stars_part(0)
    for d in range(1, group_count):
        part_copy(d).start()
    for side in range(2):

        @pl.when(has[side])
        def _(side=side):
            for copy in info_copies(1 - side):
                copy.wait_recv()
            near_lookup = look_up(1 + side)
            near_lookup.start()
            near_lookup.wait()
            stars_part(1 + side)
            for d in range(group_count):
                edge_part_copy(side, d).start()

    for d in range(1, group_count):
        main_copy(d).wait_recv()
    total = comb[me, pl.ds(PAD, rows)]
    for d in range(1, group_count):
        total = total + got_main[d - 1]
    share_ref[...] = total
    for side in range(2):

        @pl.when(has[side])
        def _(side=side):
            for d in range(group_count):
                edge_copy(1 - side, d).wait_recv()
            edge = got_edge[side, 0]
            for d in range(1, group_count):
                edge = edge + got_edge[side, d]
            share_ref[pl.ds((0, rows - PAD)[side], PAD), :] += edge

    for d in range(1, group_count):
        part_copy(d).wait_recv()
    sums = part[0]
    for d in range(1, group_count):
        sums = sums + got_part[d - 1]
    plain_ref[...] = sums[0:1]
    flagged_ref[...] = sums[1:2]
    for side in range(2):

        @pl.when(has[side])
        def _(side=side):
            for d in range(group_count):
                edge_part_copy(1 - side, d).wait_recv()
            edge = got_edge_part[side, 0]
            for d in range(1, group_count):
                edge = edge + got_edge_part[side, d]
            plain_ref[...] += edge[0:1]
            flagged_ref[...] += edge[1:2]

    for d in range(1, group_count):
        main_copy(d).wait_send()
        part_copy(d).wait_send()
    for side in range(2):

        @pl.when(has[side])
        def _(side=side):
            for copy in info_copies(side):
                copy.wait_send()
            for d in range(group_count):
                edge_copy(side, d).wait_send()
                edge_part_copy(side, d).wait_send()


def per_device(residual, point_spread, star_row, star_col, star_flux, transit_depth, transit_flag):
    times, rows, columns = residual.shape
    width = point_spread.shape[0]
    margin = (width - 1) // 2
    blocks = columns // LANES
    count = star_row.shape[0]
    groups = lax.axis_size("tm")
    share = columns // groups
    vmem = pl.BlockSpec(memory_space=pltpu.VMEM)
    anywhere = pl.BlockSpec(memory_space=pltpu.HBM)
    dma = pltpu.SemaphoreType.DMA
    grid_share, plain, flagged = pl.pallas_call(
        kernel,
        out_shape=(
            jax.ShapeDtypeStruct((rows, share), jnp.float32),
            jax.ShapeDtypeStruct((1, count), jnp.float32),
            jax.ShapeDtypeStruct((1, count), jnp.float32),
        ),
        in_specs=[anywhere] * 5,
        out_specs=(vmem, vmem, vmem),
        scratch_shapes=[
            pltpu.VMEM(point_spread.shape, point_spread.dtype),
            pltpu.VMEM(residual.shape, residual.dtype),
            pltpu.VMEM((3, 2, 1, count), jnp.int32),
            pltpu.VMEM((3, times, count), jnp.int32),
            pltpu.VMEM((3, 2, 1, count), jnp.int32),
            pltpu.SMEM((3, 2, 1, count), jnp.int32),
            pltpu.VMEM((256, columns + 2 * LANES), jnp.float32),
            pltpu.VMEM((2 * blocks * (rows + 2 * margin), 16, LANES), jnp.bfloat16),
            pltpu.VMEM((width * LANES, LANES), jnp.bfloat16),
            pltpu.VMEM((256, width * LANES), jnp.bfloat16),
            pltpu.VMEM((4, 256, width * LANES), jnp.bfloat16),
            pltpu.VMEM((4, 256, LANES), jnp.float32),
            pltpu.VMEM((rows, columns + 3 * LANES), jnp.float32),
            pltpu.VMEM((2 * rows * (share // LANES), 256), jnp.bfloat16),
            pltpu.VMEM((groups, rows + 2 * PAD, share), jnp.float32),
            pltpu.VMEM((3, 8, count), jnp.float32),
            pltpu.VMEM((groups - 1, rows, share), jnp.float32),
            pltpu.VMEM((2, groups, PAD, share), jnp.float32),
            pltpu.VMEM((groups - 1, 8, count), jnp.float32),
            pltpu.VMEM((2, groups, 8, count), jnp.float32),
            dma((2, 3)), dma((2, 3)), dma((groups - 1,)), dma((groups - 1,)),
            dma((2, groups)), dma((2, groups)), dma((groups - 1,)), dma((groups - 1,)),
            dma((2, groups)), dma((2, groups)), dma((5,)), dma((3,)),
        ],
        compiler_params=pltpu.CompilerParams(
            collective_id=0, has_side_effects=True, vmem_limit_bytes=62 << 20
        ),
    )(point_spread, residual, star_row[None], star_col[None], transit_flag)
    return grid_share, plain[0] - transit_depth * flagged[0], -star_flux * flagged[0]


def solution(mesh):
    in_specs = (P("tm", "sky", None), P(), P("sky"), P("sky"), P("sky"), P("sky"), P("tm", "sky"))
    out_specs = (P("sky", "tm"), P("sky"), P("sky"))
    return jax.shard_map(
        per_device, mesh=mesh, in_specs=in_specs, out_specs=out_specs, check_vma=False
    )
```
